32 devices in a mesh: chan: 16 (over z, x, core), tm: 2 (over y).
Axes of the slice: x: 2, y: 2, z: 4, core: 2. Of those that a mesh axis runs over, the one named last changes fastest.
Arguments:
- traces: bfloat16 [512, 4, 2048], P('chan', None, 'tm'), may hold values from -40 to 40
- delays: int32 [128, 512], P(None, 'chan'), may hold values from 0 to 1023
- offsets: int32 [4], P('tm'), may hold values from 0 to 2047
Outputs:
- brightness: float32 [4, 128, 256], P('tm', 'chan')
The draws below stay inside these ranges and needn't reach their ends.
All inputs are finite; a program needn't handle non-finite values.
Results may differ from the reference program's by a relative error of at most 0.0048.
Values may be sent and summed in bfloat16 or wider, within the bound.
A program may use at most 64 MiB of HBM per device.

```python
import math
import jax
import jax.numpy as jnp
from jax import lax

CH_DEV = 32
WINDOWS = 4
NODES_DEV = 8
SAMPLES = 2048
BAND = 512
FB = 128
TB = 256
BAND_LO = 128
DEC = 8
CHANNELS = 512
NODES = 128
N_CHAN = 16


def draw_traces(key, part):
    keys = jax.random.split(jax.random.fold_in(key, 17), 3)
    block_len = SAMPLES // 8
    channel_scale = jnp.exp(jax.random.uniform(keys[0], (CHANNELS, 1, 1, 1), jnp.float32) * math.log(10.0))
    block_scale = jnp.exp(jax.random.uniform(keys[1], (CHANNELS, WINDOWS, 8, 1), jnp.float32) * math.log(10.0))
    noise = jnp.clip(jax.random.normal(keys[2], (CHANNELS, WINDOWS, 8, block_len), jnp.float32), -4.0, 4.0)
    values = noise * block_scale * channel_scale / 10.0
    return values.reshape(CHANNELS, WINDOWS, SAMPLES).astype(jnp.bfloat16)


def set_ends(result, own_key, low, high):
    extent = result.shape
    index_at = [jax.random.randint(jax.random.fold_in(own_key, axis), (), 0, extent[axis]) for axis in range(len(extent))]
    result = result.at[tuple(index_at)].set(low)
    longest = extent.index(max(extent))
    index_at[longest] = (index_at[longest] + 1) % extent[longest]
    return result.at[tuple(index_at)].set(high)


def setup_inputs(seed: int = 0) -> dict:
    splits = jax.random.split(jax.random.key(seed), 4)
    return {
        "traces": draw_traces(jax.random.fold_in(splits[3], 71), 0),
        "delays": set_ends(jax.random.randint(splits[1], (NODES, CHANNELS), 0, SAMPLES // 2), jax.random.fold_in(splits[1], 1), 0, (SAMPLES // 2) - 1).astype(jnp.int32),
        "offsets": set_ends(jax.random.randint(splits[2], (WINDOWS,), 0, SAMPLES), jax.random.fold_in(splits[2], 1), 0, SAMPLES - 1).astype(jnp.int32),
    }


epsilon = 1e-06
full_turn = 2.0 * math.pi

def angle_grid(first_ids, second_ids):
    product = first_ids[:, None] * second_ids[None, :] % SAMPLES
    return product.astype(jnp.float32) * (full_turn / SAMPLES)

def reference(traces, delays, offsets):
    sample_ids = jnp.arange(SAMPLES, dtype=jnp.int32)
    band_bins = BAND_LO + jnp.arange(BAND, dtype=jnp.int32)
    taper = jnp.sin(jnp.pi * (jnp.arange(BAND, dtype=jnp.float32) + 0.5) / BAND) ** 2
    forward_angles = angle_grid(sample_ids, band_bins)
    forward = jnp.concatenate([jnp.cos(forward_angles), -jnp.sin(forward_angles)], axis=1).astype(jnp.bfloat16)
    back_angles = angle_grid(band_bins, sample_ids)
    weight = (2.0 * taper / SAMPLES)[:, None]
    upper = jnp.concatenate([weight * jnp.cos(back_angles), weight * jnp.sin(back_angles)], axis=1)
    lower = jnp.concatenate([-weight * jnp.sin(back_angles), weight * jnp.cos(back_angles)], axis=1)
    inverse = jnp.concatenate([upper, lower], axis=0).astype(jnp.bfloat16)
    env_bins = 1 + jnp.arange(FB, dtype=jnp.int32)
    env_angles = angle_grid(sample_ids, env_bins)
    envelope_table = jnp.concatenate([jnp.cos(env_angles), -jnp.sin(env_angles)], axis=1).astype(jnp.bfloat16)

    def process(block_traces):
        trace_rows = block_traces.reshape(CH_DEV * WINDOWS, SAMPLES)
        spectrum = jnp.dot(trace_rows, forward, preferred_element_type=jnp.float32).astype(jnp.bfloat16)
        analytic = jnp.dot(spectrum, inverse, preferred_element_type=jnp.float32)
        real_part = analytic[:, :SAMPLES]
        imag_part = analytic[:, SAMPLES:]
        energy = real_part * real_part + imag_part * imag_part
        energy_sum = lax.optimization_barrier(jnp.sum(energy, axis=1))
        envelope_spectrum = jnp.dot(energy.astype(jnp.bfloat16), envelope_table, preferred_element_type=jnp.float32)
        factor = 1.0 / (math.sqrt(SAMPLES) * (energy_sum / SAMPLES + epsilon))
        normalized = (envelope_spectrum * factor[:, None]).astype(jnp.bfloat16)
        return normalized.reshape(CH_DEV, WINDOWS, 2 * FB)
    normalized = lax.map(process, traces.reshape(N_CHAN, CH_DEV, WINDOWS, SAMPLES))
    normalized = normalized.reshape(CHANNELS, WINDOWS, 2 * FB)
    e_real = normalized[:, :, :FB]
    e_imag = normalized[:, :, FB:]
    real_block = jnp.concatenate([e_real, -e_imag], axis=0)
    imag_block = jnp.concatenate([e_imag, e_real], axis=0)
    spectra_pair = jnp.concatenate([real_block, imag_block], axis=1).astype(jnp.float32)

    def stack_block(delay_rows):
        product = delay_rows[:, :, None] * env_bins[None, None, :] % SAMPLES
        angles = product.astype(jnp.float32) * (full_turn / SAMPLES)
        phase = jnp.concatenate([jnp.cos(angles), jnp.sin(angles)], axis=1).astype(jnp.bfloat16)
        return jnp.einsum('ncf,cwf->nwf', phase.astype(jnp.float32), spectra_pair)
    stacks = lax.map(stack_block, delays.reshape(N_CHAN, NODES_DEV, CHANNELS))
    stacks = stacks.reshape(NODES, 2, WINDOWS, FB)
    out_times = offsets[:, None] + DEC * jnp.arange(TB, dtype=jnp.int32)[None, :]
    product = env_bins[None, :, None] * out_times[:, None, :] % SAMPLES
    out_angles = product.astype(jnp.float32) * (full_turn / SAMPLES)
    scale = 1.0 / math.sqrt(FB * CHANNELS)
    bright = jnp.einsum('nwf,wfk->wnk', stacks[:, 0], jnp.cos(out_angles), precision=lax.Precision.HIGHEST)
    bright = bright - jnp.einsum('nwf,wfk->wnk', stacks[:, 1], jnp.sin(out_angles), precision=lax.Precision.HIGHEST)
    return bright * scale
```

```python
import functools
import math

import jax
import jax.numpy as jnp
from jax import lax
from jax.experimental import pallas as pl
from jax.experimental.pallas import tpu as pltpu
from jax.sharding import PartitionSpec as P

SAMPLES = 2048
BAND = 512
FB = 128
TB = 256
BAND_LO = 128
DEC = 8
STEP = 32
PAIR = 2

epsilon = 1e-06
full_turn = 2.0 * math.pi
MESH = pl.DeviceIdType.MESH


def cos_sin(index):
    quarter = SAMPLES // 4
    turn = (index + quarter // 2) >> 9
    x = (index - (turn << 9)).astype(jnp.float32) * (full_turn / SAMPLES)
    y = x * x
    s = x + x * y * (-1.6666654611e-1 + y * (8.3321608736e-3 + y * -1.9515295891e-4))
    c = 1.0 - 0.5 * y + y * y * (
        4.166664568298827e-2 + y * (-1.388731625493765e-3 + y * 2.443315711809948e-5)
    )
    odd = (turn & 1) != 0
    cos_part = jnp.where(odd, s, c)
    sin_part = jnp.where(odd, c, s)
    cos_out = jnp.where(((turn + 1) & 2) != 0, -cos_part, cos_part)
    sin_out = jnp.where((turn & 2) != 0, -sin_part, sin_part)
    return cos_out, sin_out


def parity_row(first, width):
    ids = first + lax.broadcasted_iota(jnp.int32, (1, width), 1)
    return (1 - 2 * (ids & 1)).astype(jnp.float32)


def kernel(
    n_chan, x_ref, d_ref, off_ref, out_ref,
    other, base_c, base_s, lead_c, lead_s, fwd, inv, env, phase_c, phase_s,
    nodes_d, turn_tab, spec, e_tab, send_buf, recv_buf,
    x_send, x_recv, send_sem, recv_sem,
):
    windows, chans, half = x_ref.shape
    kept = windows // 2
    rows = kept * chans
    nodes = d_ref.shape[1]
    node_rows = nodes // n_chan
    me = lax.axis_index("chan")
    tm = lax.axis_index("tm")
    partner = 1 - tm

    barrier = pltpu.get_barrier_semaphore()
    pl.semaphore_signal(barrier, inc=1, device_id={"tm": partner}, device_id_type=MESH)

    @pl.loop(1, n_chan)
    def _(step):
        pl.semaphore_signal(
            barrier, inc=1, device_id={"chan": lax.rem(me + step, n_chan)}, device_id_type=MESH
        )

    width = BAND + FB
    lane = lax.broadcasted_iota(jnp.int32, (STEP, width), 1)
    row = lax.broadcasted_iota(jnp.int32, (STEP, width), 0)
    freq = jnp.where(lane < BAND, lane + BAND_LO, lane - BAND + 1)
    c, s = cos_sin((freq * row) & (SAMPLES - 1))
    base_c[...] = c
    base_s[...] = s
    leads = half // STEP
    for q in range(width // 128):
        first = (BAND_LO if q * 128 < BAND else 1 - BAND) + q * 128
        ids = first + lax.broadcasted_iota(jnp.int32, (leads, 128), 1)
        leap = STEP * lax.broadcasted_iota(jnp.int32, (leads, 128), 0)
        c, s = cos_sin((ids * leap) & (SAMPLES - 1))
        lead_c[q] = c
        lead_s[q] = s

    taper_angle = math.pi * (lax.broadcasted_iota(jnp.int32, (1, BAND), 1).astype(jnp.float32) + 0.5) / BAND
    weight = 2.0 * jnp.sin(taper_angle) ** 2 / SAMPLES

    @pl.loop(0, half // STEP)
    def _(a):
        at = pl.ds(pl.multiple_of(a * STEP, STEP), STEP)
        for q in range(width // 128):
            cols = slice(q * 128, (q + 1) * 128)
            ca, sa = lead_c[q, pl.ds(a, 1), :], lead_s[q, pl.ds(a, 1), :]
            cb, sb = base_c[:, cols], base_s[:, cols]
            c = ca * cb - sa * sb
            s = sa * cb + ca * sb
            if q * 128 < BAND:
                g = weight[:, cols]
                high = slice(BAND + q * 128, BAND + (q + 1) * 128)
                fwd[at, cols] = c.astype(jnp.bfloat16)
                fwd[at, high] = (-s).astype(jnp.bfloat16)
                inv[at, cols] = (g * c).astype(jnp.bfloat16)
                inv[at, high] = (g * s).astype(jnp.bfloat16)
            else:
                low = slice(q * 128 - BAND, (q + 1) * 128 - BAND)
                high = slice(FB + low.start, FB + low.stop)
                env[at, low] = c.astype(jnp.bfloat16)
                env[at, high] = (-s).astype(jnp.bfloat16)

    pl.semaphore_wait(barrier, n_chan)
    exchange = pltpu.make_async_remote_copy(
        src_ref=x_ref.at[pl.ds(partner * kept, kept)],
        dst_ref=other,
        send_sem=x_send,
        recv_sem=x_recv,
        device_id={"tm": partner},
        device_id_type=MESH,
    )
    exchange.start()

    nodes_d[...] = d_ref[...].T
    block = PAIR * node_rows
    env_bins = 1 + lax.broadcasted_iota(jnp.int32, (block, FB), 1)

    @pl.loop(0, nodes // block)
    def _(b):
        at = pl.ds(pl.multiple_of(b * block, block), block)
        delay = nodes_d[at, :]
        for ch in range(chans):
            c, s = cos_sin((delay[:, ch : ch + 1] * env_bins) & (SAMPLES - 1))
            phase_c[ch, at, :] = c.astype(jnp.bfloat16)
            phase_s[ch, at, :] = s.astype(jnp.bfloat16)

    f_col = 1 + lax.broadcasted_iota(jnp.int32, (FB, TB), 0)
    k_row = lax.broadcasted_iota(jnp.int32, (FB, TB), 1)
    c, s = cos_sin((f_col * k_row * DEC) & (SAMPLES - 1))
    turn_tab[:FB, :] = c
    turn_tab[FB:, :] = -s

    exchange.wait()

    own = x_ref[pl.ds(tm * kept, kept)].reshape(rows, half)
    own_terms = jnp.dot(own, fwd[...], preferred_element_type=jnp.float32)
    other_terms = jnp.dot(other[...].reshape(rows, half), fwd[...], preferred_element_type=jnp.float32)
    band_sign = parity_row(BAND_LO, 2 * BAND)
    is_late = (lax.broadcasted_iota(jnp.int32, (1, 2 * BAND), 1) * 0 + tm) == 1
    own_sign = jnp.where(is_late, band_sign, 1.0)
    other_sign = jnp.where(is_late, 1.0, band_sign)
    total = (own_terms * own_sign + other_terms * other_sign).astype(jnp.bfloat16).astype(jnp.float32)
    re, im = total[:, :BAND], total[:, BAND:]
    sign = band_sign[:, :BAND]
    for at, value in enumerate((re, re * sign, im, im * sign)):
        spec[at * rows : (at + 1) * rows, :BAND] = value.astype(jnp.bfloat16)
    for at, value in enumerate((-im, -im * sign, re, re * sign)):
        spec[at * rows : (at + 1) * rows, BAND:] = value.astype(jnp.bfloat16)
    analytic = lax.dot_general(
        spec[...], inv[...], (((1,), (1,)), ((), ())), preferred_element_type=jnp.float32
    )
    real_part, imag_part = analytic[: 2 * rows], analytic[2 * rows :]
    energy = real_part * real_part + imag_part * imag_part
    sums = jnp.sum(energy, axis=1, keepdims=True)
    sums = sums[:rows] + sums[rows:]
    spread = jnp.dot(energy.astype(jnp.bfloat16), env[...], preferred_element_type=jnp.float32)
    spread = spread[:rows] + spread[rows:] * parity_row(1, 2 * FB)
    factor = 1.0 / (math.sqrt(SAMPLES) * (sums / SAMPLES + epsilon))
    e_tab[...] = (spread * factor).astype(jnp.bfloat16).astype(jnp.float32)

    pairs = n_chan // PAIR
    my_pair = me // PAIR

    def pair_at(step):
        return lax.rem(my_pair + 1 + step, pairs)

    def outgoing(dest):
        return pltpu.make_async_remote_copy(
            src_ref=send_buf.at[dest],
            dst_ref=recv_buf.at[me],
            send_sem=send_sem.at[dest],
            recv_sem=recv_sem.at[me],
            device_id={"chan": dest},
            device_id_type=MESH,
        )

    def send_pair(step):
        for side in range(PAIR):
            dest = pair_at(step) * PAIR + side

            @pl.when(dest != me)
            def _():
                outgoing(dest).start()

    @pl.loop(0, pairs)
    def _(step):
        pair = pair_at(step)
        at = pl.ds(pl.multiple_of(pair * block, block), block)
        acc = [[jnp.zeros((block, FB), jnp.float32) for _ in range(kept)] for _ in range(2)]
        for ch in range(chans):
            pc = phase_c[ch, at, :].astype(jnp.float32)
            ps = phase_s[ch, at, :].astype(jnp.float32)
            for w in range(kept):
                r = w * chans + ch
                er, ei = e_tab[r : r + 1, :FB], e_tab[r : r + 1, FB:]
                acc[0][w] = acc[0][w] + (pc * er - ps * ei)
                acc[1][w] = acc[1][w] + (pc * ei + ps * er)
        for side in range(PAIR):
            part = slice(side * node_rows, (side + 1) * node_rows)
            packed = jnp.concatenate([acc[p][w][part] for p in range(2) for w in range(kept)], axis=0)
            send_buf[pair * PAIR + side] = packed.astype(jnp.bfloat16)

        @pl.when(step > 0)
        def _():
            send_pair(step - 1)

    send_pair(pairs - 1)

    def incoming(source):
        return pltpu.make_async_remote_copy(
            src_ref=send_buf.at[source],
            dst_ref=recv_buf.at[source],
            send_sem=send_sem.at[source],
            recv_sem=recv_sem.at[source],
            device_id={"chan": source},
            device_id_type=MESH,
        )

    def add_in(step, stack):
        source = lax.rem(me + n_chan - step, n_chan)
        incoming(source).wait_recv()
        return stack + recv_buf[source].astype(jnp.float32)

    stack = lax.fori_loop(1, n_chan, add_in, send_buf[me].astype(jnp.float32))

    bins = 1 + lax.broadcasted_iota(jnp.int32, (1, FB), 1)
    turned = []
    for w in range(kept):
        c, s = cos_sin((bins * off_ref[w]) & (SAMPLES - 1))
        re = stack[w * node_rows : (w + 1) * node_rows]
        im = stack[(kept + w) * node_rows : (kept + w + 1) * node_rows]
        turned.append(jnp.concatenate([re * c - im * s, re * s + im * c], axis=1))
    bright = jnp.dot(
        jnp.concatenate(turned, axis=0), turn_tab[...],
        precision=lax.Precision.HIGHEST, preferred_element_type=jnp.float32,
    )
    scale = 1.0 / math.sqrt(FB * chans * n_chan)
    out_ref[...] = (bright * scale).reshape(kept, node_rows, TB)

    @pl.loop(1, n_chan)
    def _(step):
        outgoing(lax.rem(me + step, n_chan)).wait_send()


def solution(mesh):
    n_chan = mesh.shape["chan"]

    def on_device(traces, delays, offsets):
        chans, windows, half = traces.shape
        nodes = delays.shape[0]
        kept = offsets.shape[0]
        node_rows = nodes // n_chan
        by_window = jnp.transpose(traces, (1, 0, 2))
        vmem = pl.BlockSpec(memory_space=pltpu.VMEM)
        packed_rows = 2 * kept * node_rows
        return pl.pallas_call(
            functools.partial(kernel, n_chan),
            out_shape=jax.ShapeDtypeStruct((kept, node_rows, TB), jnp.float32),
            in_specs=[vmem, vmem, pl.BlockSpec(memory_space=pltpu.SMEM)],
            out_specs=vmem,
            scratch_shapes=[
                pltpu.VMEM((kept, chans, half), jnp.bfloat16),
                pltpu.VMEM((STEP, BAND + FB), jnp.float32),
                pltpu.VMEM((STEP, BAND + FB), jnp.float32),
                pltpu.VMEM(((BAND + FB) // 128, half // STEP, 128), jnp.float32),
                pltpu.VMEM(((BAND + FB) // 128, half // STEP, 128), jnp.float32),
                pltpu.VMEM((half, 2 * BAND), jnp.bfloat16),
                pltpu.VMEM((half, 2 * BAND), jnp.bfloat16),
                pltpu.VMEM((half, 2 * FB), jnp.bfloat16),
                pltpu.VMEM((chans, nodes, FB), jnp.bfloat16),
                pltpu.VMEM((chans, nodes, FB), jnp.bfloat16),
                pltpu.VMEM((nodes, chans), jnp.int32),
                pltpu.VMEM((2 * FB, TB), jnp.float32),
                pltpu.VMEM((4 * kept * chans, 2 * BAND), jnp.bfloat16),
                pltpu.VMEM((kept * chans, 2 * FB), jnp.float32),
                pltpu.VMEM((n_chan, packed_rows, FB), jnp.bfloat16),
                pltpu.VMEM((n_chan, packed_rows, FB), jnp.bfloat16),
                pltpu.SemaphoreType.DMA,
                pltpu.SemaphoreType.DMA,
                pltpu.SemaphoreType.DMA((n_chan,)),
                pltpu.SemaphoreType.DMA((n_chan,)),
            ],
            compiler_params=pltpu.CompilerParams(
                collective_id=0, has_side_effects=True, vmem_limit_bytes=56 * 1024 * 1024
            ),
        )(by_window, delays.T, offsets)

    placed = (P("chan", None, "tm"), P(None, "chan"), P("tm"))
    return jax.shard_map(
        on_device, mesh=mesh, in_specs=placed, out_specs=P("tm", "chan", None), check_vma=False
    )
```

```python
import functools
import math

import jax
import jax.numpy as jnp
from jax import lax
from jax.experimental import pallas as pl
from jax.experimental.pallas import tpu as pltpu
from jax.sharding import PartitionSpec as P

SAMPLES = 2048
BAND = 512
FB = 128
TB = 256
BAND_LO = 128
DEC = 8
STEP = 32
PAIR = 2

epsilon = 1e-06
full_turn = 2.0 * math.pi
MESH = pl.DeviceIdType.MESH


COS_TURN = (
    0.9999999890590201, -19.739204499453688, 64.93911745988827, -85.45013953077586,
    60.16763095018129, -25.96759924584206, 6.528658157862129,
)
SIN_TURN = (
    6.283185302511498, -41.341700405316736, 81.60513138576982, -76.70301535347629,
    42.02592698341473, -14.899846660399582, 3.2381375010236435,
)


def cos_sin(turns):
    x = turns - jnp.round(turns)
    y = x * x
    c, s = COS_TURN[-1], SIN_TURN[-1]
    for c_next, s_next in zip(COS_TURN[-2::-1], SIN_TURN[-2::-1]):
        c = c * y + c_next
        s = s * y + s_next
    return c, s * x


def float_iota(shape, axis):
    return lax.broadcasted_iota(jnp.int32, shape, axis).astype(jnp.float32)


def bit_of(value, at):
    return lax.rem(value // (1 << at), 2)


def flip(value, at):
    return value + (1 - 2 * bit_of(value, at)) * (1 << at)


def parity_row(first, width):
    ids = first + lax.broadcasted_iota(jnp.int32, (1, width), 1)
    return (1 - 2 * (ids & 1)).astype(jnp.float32)


def kernel(
    n_chan, x_ref, d_ref, off_ref, out_ref,
    other, base_c, base_s, lead_c, lead_s, fwd, inv, env, phase_c, phase_s,
    nodes_d, turn_tab, turn_row, spec, e_tab, send_buf, recv_buf,
    x_send, x_recv, send_sem, recv_sem, round_sem,
):
    windows, chans, half = x_ref.shape
    kept = windows // 2
    rows = kept * chans
    nodes = d_ref.shape[1]
    node_rows = nodes // n_chan
    me = lax.axis_index("chan")
    tm = lax.axis_index("tm")
    partner = 1 - tm

    rounds = n_chan.bit_length() - 1
    barrier = pltpu.get_barrier_semaphore()
    pl.semaphore_signal(barrier, inc=1, device_id={"tm": partner}, device_id_type=MESH)
    for r in range(rounds):
        pl.semaphore_signal(barrier, inc=1, device_id={"chan": flip(me, r)}, device_id_type=MESH)

    def tell(r):
        if r < rounds:
            pl.semaphore_signal(round_sem.at[r], inc=1, device_id={"chan": flip(me, r)}, device_id_type=MESH)

    def hear(r):
        if r < rounds:
            pl.semaphore_wait(round_sem.at[r], 1)
            tell(r + 1)

    width = BAND + FB
    leads = half // STEP
    unit = 1.0 / SAMPLES
    for q in range(width // 128):
        cols = slice(q * 128, (q + 1) * 128)
        first = (BAND_LO if q * 128 < BAND else 1 - BAND) + q * 128
        freq = (float_iota((1, 128), 1) + first) * unit
        base_c[:, cols], base_s[:, cols] = cos_sin(float_iota((STEP, 128), 0) * freq)
        lead_c[q], lead_s[q] = cos_sin(float_iota((leads, 128), 0) * (freq * STEP))

    taper_angle = math.pi * (lax.broadcasted_iota(jnp.int32, (1, BAND), 1).astype(jnp.float32) + 0.5) / BAND
    weight = 2.0 * jnp.sin(taper_angle) ** 2 / SAMPLES

    pl.semaphore_wait(barrier, rounds + 1)
    exchange = pltpu.make_async_remote_copy(
        src_ref=x_ref.at[pl.ds(partner * kept, kept)],
        dst_ref=other,
        send_sem=x_send,
        recv_sem=x_recv,
        device_id={"tm": partner},
        device_id_type=MESH,
    )
    exchange.start()

    tell(0)

    @pl.loop(0, half // STEP)
    def _(a):
        at = pl.ds(pl.multiple_of(a * STEP, STEP), STEP)
        for q in range(width // 128):
            cols = slice(q * 128, (q + 1) * 128)
            ca, sa = lead_c[q, pl.ds(a, 1), :], lead_s[q, pl.ds(a, 1), :]
            cb, sb = base_c[:, cols], base_s[:, cols]
            c = ca * cb - sa * sb
            s = sa * cb + ca * sb
            if q * 128 < BAND:
                g = weight[:, cols]
                high = slice(BAND + q * 128, BAND + (q + 1) * 128)
                fwd[at, cols] = c.astype(jnp.bfloat16)
                fwd[at, high] = (-s).astype(jnp.bfloat16)
                inv[at, cols] = (g * c).astype(jnp.bfloat16)
                inv[at, high] = (g * s).astype(jnp.bfloat16)
            else:
                low = slice(q * 128 - BAND, (q + 1) * 128 - BAND)
                high = slice(FB + low.start, FB + low.stop)
                env[at, low] = c.astype(jnp.bfloat16)
                env[at, high] = (-s).astype(jnp.bfloat16)

    hear(0)

    nodes_d[...] = (d_ref[...].astype(jnp.float32) * unit).T
    block = PAIR * node_rows
    env_bins = 1.0 + float_iota((1, FB), 1)

    @pl.loop(0, nodes // block)
    def _(b):
        at = pl.ds(pl.multiple_of(b * block, block), block)
        delay = nodes_d[at, :]
        for ch in range(chans):
            c, s = cos_sin(delay[:, ch : ch + 1] * env_bins)
            phase_c[ch, at, :] = c.astype(jnp.bfloat16)
            phase_s[ch, at, :] = s.astype(jnp.bfloat16)

    hear(1)
    c, s = cos_sin((1.0 + float_iota((FB, TB), 0)) * (float_iota((FB, TB), 1) * (DEC * unit)))
    turn_tab[:FB, :] = c
    turn_tab[FB:, :] = -s
    for w in range(kept):
        shift = off_ref[w].astype(jnp.float32) * unit
        turn_row[w, :, :FB], turn_row[w, :, FB:] = cos_sin(env_bins * shift)
    hear(2)

    own = x_ref[pl.ds(tm * kept, kept)].reshape(rows, half)
    own_terms = jnp.dot(own, fwd[...], preferred_element_type=jnp.float32)
    exchange.wait()
    other_terms = jnp.dot(other[...].reshape(rows, half), fwd[...], preferred_element_type=jnp.float32)
    band_sign = parity_row(BAND_LO, 2 * BAND)
    is_late = (lax.broadcasted_iota(jnp.int32, (1, 2 * BAND), 1) * 0 + tm) == 1
    own_sign = jnp.where(is_late, band_sign, 1.0)
    other_sign = jnp.where(is_late, 1.0, band_sign)
    total = (own_terms * own_sign + other_terms * other_sign).astype(jnp.bfloat16).astype(jnp.float32)
    re, im = total[:, :BAND], total[:, BAND:]
    sign = band_sign[:, :BAND]
    for at, value in enumerate((re, re * sign, im, im * sign)):
        spec[at * rows : (at + 1) * rows, :BAND] = value.astype(jnp.bfloat16)
    for at, value in enumerate((-im, -im * sign, re, re * sign)):
        spec[at * rows : (at + 1) * rows, BAND:] = value.astype(jnp.bfloat16)
    analytic = lax.dot_general(
        spec[...], inv[...], (((1,), (1,)), ((), ())), preferred_element_type=jnp.float32
    )
    real_part, imag_part = analytic[: 2 * rows], analytic[2 * rows :]
    energy = real_part * real_part + imag_part * imag_part
    sums = jnp.sum(energy, axis=1, keepdims=True)
    sums = sums[:rows] + sums[rows:]
    spread = jnp.dot(energy.astype(jnp.bfloat16), env[...], preferred_element_type=jnp.float32)
    spread = spread[:rows] + spread[rows:] * parity_row(1, 2 * FB)
    factor = 1.0 / (math.sqrt(SAMPLES) * (sums / SAMPLES + epsilon))
    e_tab[...] = (spread * factor).astype(jnp.bfloat16).astype(jnp.float32)

    for r in range(3, rounds):
        hear(r)

    pairs = n_chan // PAIR
    my_pair = me // PAIR

    def pair_at(step):
        mask = pairs - 1 - step
        found = 0
        for at in range(rounds - 1):
            found = found + lax.rem(bit_of(my_pair, at) + bit_of(mask, at), 2) * (1 << at)
        return found

    def outgoing(dest):
        return pltpu.make_async_remote_copy(
            src_ref=send_buf.at[dest],
            dst_ref=recv_buf.at[me],
            send_sem=send_sem.at[dest],
            recv_sem=recv_sem.at[me],
            device_id={"chan": dest},
            device_id_type=MESH,
        )

    def send_pair(step):
        for side in range(PAIR):
            dest = pair_at(step) * PAIR + side

            @pl.when(dest != me)
            def _():
                outgoing(dest).start()

    @pl.loop(0, pairs)
    def _(step):
        pair = pair_at(step)
        at = pl.ds(pl.multiple_of(pair * block, block), block)
        acc = [[jnp.zeros((block, FB), jnp.float32) for _ in range(kept)] for _ in range(2)]
        for ch in range(chans):
            pc = phase_c[ch, at, :].astype(jnp.float32)
            ps = phase_s[ch, at, :].astype(jnp.float32)
            for w in range(kept):
                r = w * chans + ch
                er, ei = e_tab[r : r + 1, :FB], e_tab[r : r + 1, FB:]
                acc[0][w] = acc[0][w] + (pc * er - ps * ei)
                acc[1][w] = acc[1][w] + (pc * ei + ps * er)
        for side in range(PAIR):
            part = slice(side * node_rows, (side + 1) * node_rows)
            packed = jnp.concatenate([acc[p][w][part] for p in range(2) for w in range(kept)], axis=0)
            send_buf[pair * PAIR + side] = packed.astype(jnp.bfloat16)

        @pl.when(step > 0)
        def _():
            send_pair(step - 1)

    send_pair(pairs - 1)

    def incoming(source):
        return pltpu.make_async_remote_copy(
            src_ref=send_buf.at[source],
            dst_ref=recv_buf.at[source],
            send_sem=send_sem.at[source],
            recv_sem=recv_sem.at[source],
            device_id={"chan": source},
            device_id_type=MESH,
        )

    def add_one(source, stack):
        incoming(source).wait_recv()
        return stack + recv_buf[source].astype(jnp.float32)

    def add_pair(step, stack):
        for side in range(PAIR):
            stack = add_one(pair_at(step) * PAIR + side, stack)
        return stack

    stack = lax.fori_loop(0, pairs - 1, add_pair, send_buf[me].astype(jnp.float32))
    stack = add_one(flip(me, 0), stack)

    turned = []
    for w in range(kept):
        c, s = turn_row[w, :, :FB], turn_row[w, :, FB:]
        re = stack[w * node_rows : (w + 1) * node_rows]
        im = stack[(kept + w) * node_rows : (kept + w + 1) * node_rows]
        turned.append(jnp.concatenate([re * c - im * s, re * s + im * c], axis=1))
    bright = jnp.dot(
        jnp.concatenate(turned, axis=0), turn_tab[...],
        precision=lax.Precision.HIGHEST, preferred_element_type=jnp.float32,
    )
    scale = 1.0 / math.sqrt(FB * chans * n_chan)
    out_ref[...] = (bright * scale).reshape(kept, node_rows, TB)

    @pl.loop(1, n_chan)
    def _(step):
        outgoing(lax.rem(me + step, n_chan)).wait_send()


def solution(mesh):
    n_chan = mesh.shape["chan"]

    def on_device(traces, delays, offsets):
        chans, windows, half = traces.shape
        nodes = delays.shape[0]
        kept = offsets.shape[0]
        node_rows = nodes // n_chan
        by_window = jnp.transpose(traces, (1, 0, 2))
        vmem = pl.BlockSpec(memory_space=pltpu.VMEM)
        packed_rows = 2 * kept * node_rows
        return pl.pallas_call(
            functools.partial(kernel, n_chan),
            out_shape=jax.ShapeDtypeStruct((kept, node_rows, TB), jnp.float32),
            in_specs=[vmem, vmem, pl.BlockSpec(memory_space=pltpu.SMEM)],
            out_specs=vmem,
            scratch_shapes=[
                pltpu.VMEM((kept, chans, half), jnp.bfloat16),
                pltpu.VMEM((STEP, BAND + FB), jnp.float32),
                pltpu.VMEM((STEP, BAND + FB), jnp.float32),
                pltpu.VMEM(((BAND + FB) // 128, half // STEP, 128), jnp.float32),
                pltpu.VMEM(((BAND + FB) // 128, half // STEP, 128), jnp.float32),
                pltpu.VMEM((half, 2 * BAND), jnp.bfloat16),
                pltpu.VMEM((half, 2 * BAND), jnp.bfloat16),
                pltpu.VMEM((half, 2 * FB), jnp.bfloat16),
                pltpu.VMEM((chans, nodes, FB), jnp.bfloat16),
                pltpu.VMEM((chans, nodes, FB), jnp.bfloat16),
                pltpu.VMEM((nodes, chans), jnp.float32),
                pltpu.VMEM((2 * FB, TB), jnp.float32),
                pltpu.VMEM((kept, 1, 2 * FB), jnp.float32),
                pltpu.VMEM((4 * kept * chans, 2 * BAND), jnp.bfloat16),
                pltpu.VMEM((kept * chans, 2 * FB), jnp.float32),
                pltpu.VMEM((n_chan, packed_rows, FB), jnp.bfloat16),
                pltpu.VMEM((n_chan, packed_rows, FB), jnp.bfloat16),
                pltpu.SemaphoreType.DMA,
                pltpu.SemaphoreType.DMA,
                pltpu.SemaphoreType.DMA((n_chan,)),
                pltpu.SemaphoreType.DMA((n_chan,)),
                pltpu.SemaphoreType.REGULAR((n_chan.bit_length() - 1,)),
            ],
            compiler_params=pltpu.CompilerParams(
                collective_id=0, has_side_effects=True, vmem_limit_bytes=16 * 1024 * 1024 + 4 * chans * nodes * FB
            ),
        )(by_window, delays.T, offsets)

    placed = (P("chan", None, "tm"), P(None, "chan"), P("tm"))
    return jax.shard_map(
        on_device, mesh=mesh, in_specs=placed, out_specs=P("tm", "chan", None), check_vma=False
    )
```

```python
import functools
import math

import jax
import jax.numpy as jnp
from jax import lax
from jax.experimental import pallas as pl
from jax.experimental.pallas import tpu as pltpu
from jax.sharding import PartitionSpec as P

SAMPLES = 2048
BAND = 512
FB = 128
TB = 256
BAND_LO = 128
DEC = 8
STEP = 32
PAIR = 2

epsilon = 1e-06
full_turn = 2.0 * math.pi
MESH = pl.DeviceIdType.MESH


COS_TURN = (
    0.9999999890590201, -19.739204499453688, 64.93911745988827, -85.45013953077586,
    60.16763095018129, -25.96759924584206, 6.528658157862129,
)
SIN_TURN = (
    6.283185302511498, -41.341700405316736, 81.60513138576982, -76.70301535347629,
    42.02592698341473, -14.899846660399582, 3.2381375010236435,
)


def cos_sin(turns):
    x = turns - jnp.round(turns)
    y = x * x
    c, s = COS_TURN[-1], SIN_TURN[-1]
    for c_next, s_next in zip(COS_TURN[-2::-1], SIN_TURN[-2::-1]):
        c = c * y + c_next
        s = s * y + s_next
    return c, s * x


def float_iota(shape, axis):
    return lax.broadcasted_iota(jnp.int32, shape, axis).astype(jnp.float32)


def bit_of(value, at):
    return lax.rem(value // (1 << at), 2)


def flip(value, at):
    return value + (1 - 2 * bit_of(value, at)) * (1 << at)


def parity_row(first, width):
    ids = first + lax.broadcasted_iota(jnp.int32, (1, width), 1)
    return (1 - 2 * (ids & 1)).astype(jnp.float32)


def kernel(
    n_chan, x_ref, d_ref, off_hbm, out_ref,
    other, base_c, base_s, lead_c, lead_s, fwd, inv, env, phase_c, phase_s,
    nodes_d, turn_tab, turn_row, e_tab, send_buf, recv_buf,
    off_ref, off_sem, x_send, x_recv, send_sem, recv_sem, round_sem,
):
    windows, chans, half = x_ref.shape
    kept = windows // 2
    rows = kept * chans
    nodes = d_ref.shape[1]
    node_rows = nodes // n_chan
    me = lax.axis_index("chan")
    tm = lax.axis_index("tm")
    partner = 1 - tm

    offsets_in = pltpu.make_async_copy(off_hbm, off_ref, off_sem)
    offsets_in.start()

    rounds = n_chan.bit_length() - 1
    barrier = pltpu.get_barrier_semaphore()
    pl.semaphore_signal(barrier, inc=1, device_id={"tm": partner}, device_id_type=MESH)
    for r in range(rounds):
        pl.semaphore_signal(barrier, inc=1, device_id={"chan": flip(me, r)}, device_id_type=MESH)

    def tell(r):
        if r < rounds:
            pl.semaphore_signal(round_sem.at[r], inc=1, device_id={"chan": flip(me, r)}, device_id_type=MESH)

    def hear(r):
        if r < rounds:
            pl.semaphore_wait(round_sem.at[r], 1)
            tell(r + 1)

    width = BAND + FB
    tiles = BAND // 128
    side_tiles = tiles // 2
    side_band = BAND // 2
    leads = half // STEP
    unit = 1.0 / SAMPLES
    for q in range(width // 128):
        cols = slice(q * 128, (q + 1) * 128)
        if q < tiles:
            freq = (2.0 * float_iota((1, 128), 1) + (BAND_LO + q % side_tiles * 256 + q // side_tiles)) * unit
        else:
            freq = (float_iota((1, 128), 1) + (1 + (q - tiles) * 128)) * unit
        base_c[:, cols], base_s[:, cols] = cos_sin(float_iota((STEP, 128), 0) * freq)
        lead_c[q], lead_s[q] = cos_sin(float_iota((leads, 128), 0) * (freq * STEP))

    place = float_iota((1, side_band), 1) * 2.0
    place = jnp.concatenate([place, place + 1.0], axis=1)
    taper_angle = math.pi * (place + 0.5) / BAND
    weight = 2.0 * jnp.sin(taper_angle) ** 2 / SAMPLES

    pl.semaphore_wait(barrier, rounds + 1)
    exchange = pltpu.make_async_remote_copy(
        src_ref=x_ref.at[pl.ds(partner * kept, kept)],
        dst_ref=other,
        send_sem=x_send,
        recv_sem=x_recv,
        device_id={"tm": partner},
        device_id_type=MESH,
    )
    exchange.start()

    tell(0)

    @pl.loop(0, half // STEP)
    def _(a):
        at = pl.ds(pl.multiple_of(a * STEP, STEP), STEP)
        for q in range(width // 128):
            cols = slice(q * 128, (q + 1) * 128)
            ca, sa = lead_c[q, pl.ds(a, 1), :], lead_s[q, pl.ds(a, 1), :]
            cb, sb = base_c[:, cols], base_s[:, cols]
            c = ca * cb - sa * sb
            s = sa * cb + ca * sb
            if q * 128 < BAND:
                g = weight[:, cols]
                high = slice(BAND + q * 128, BAND + (q + 1) * 128)
                fwd[at, cols] = c.astype(jnp.bfloat16)
                fwd[at, high] = (-s).astype(jnp.bfloat16)
                to = q // side_tiles * BAND + q % side_tiles * 128
                inv[at, to : to + 128] = (g * c).astype(jnp.bfloat16)
                inv[at, to + side_band : to + side_band + 128] = (g * s).astype(jnp.bfloat16)
            else:
                low = slice(q * 128 - BAND, (q + 1) * 128 - BAND)
                high = slice(FB + low.start, FB + low.stop)
                env[at, low] = c.astype(jnp.bfloat16)
                env[at, high] = (-s).astype(jnp.bfloat16)

    hear(0)

    nodes_d[...] = (d_ref[...].astype(jnp.float32) * unit).T
    block = PAIR * node_rows
    env_bins = 1.0 + float_iota((1, FB), 1)

    pairs = n_chan // PAIR
    ahead = (pairs + 1) // 2
    my_pair = me // PAIR

    def pair_at(step):
        mask = pairs - 1 - step
        found = 0
        for at in range(rounds - 1):
            found = found + lax.rem(bit_of(my_pair, at) + bit_of(mask, at), 2) * (1 << at)
        return found

    def phases(step):
        at = pl.ds(pl.multiple_of(pair_at(step) * block, block), block)
        delay = nodes_d[at, :]
        for ch in range(chans):
            c, s = cos_sin(delay[:, ch : ch + 1] * env_bins)
            phase_c[ch, at, :] = c.astype(jnp.bfloat16)
            phase_s[ch, at, :] = s.astype(jnp.bfloat16)

    pl.loop(0, ahead)(phases)
    hear(1)
    c, s = cos_sin((1.0 + float_iota((FB, TB), 0)) * (float_iota((FB, TB), 1) * (DEC * unit)))
    turn_tab[:FB, :] = c
    turn_tab[FB:, :] = -s
    offsets_in.wait()
    for w in range(kept):
        shift = off_ref[w].astype(jnp.float32) * unit
        turn_row[w, :, :FB], turn_row[w, :, FB:] = cos_sin(env_bins * shift)
    hear(2)

    own = x_ref[pl.ds(tm * kept, kept)].reshape(rows, half)
    own_terms = jnp.dot(own, fwd[...], preferred_element_type=jnp.float32)
    exchange.wait()
    other_terms = jnp.dot(other[...].reshape(rows, half), fwd[...], preferred_element_type=jnp.float32)
    late_sign = jnp.where((lax.broadcasted_iota(jnp.int32, (1, side_band), 1) * 0 + tm) == 1, -1.0, 1.0)

    def spectrum(first, odd):
        cols = slice(first, first + side_band)
        mine, theirs = own_terms[:, cols], other_terms[:, cols]
        both = (mine - theirs) * late_sign if odd else mine + theirs
        return both.astype(jnp.bfloat16).astype(jnp.float32)

    def analytic(odd):
        re, im = spectrum(odd * side_band, odd), spectrum(BAND + odd * side_band, odd)
        left = jnp.concatenate([re, im], axis=0)
        right = jnp.concatenate([-im, re], axis=0)
        return lax.dot_general(
            jnp.concatenate([left, right], axis=1).astype(jnp.bfloat16),
            inv[:, odd * BAND : (odd + 1) * BAND],
            (((1,), (1,)), ((), ())),
            preferred_element_type=jnp.float32,
        )

    even_part, odd_part = analytic(0), analytic(1)
    early, late = even_part + odd_part, even_part - odd_part
    real_part = jnp.concatenate([early[:rows], late[:rows]], axis=0)
    imag_part = jnp.concatenate([early[rows:], late[rows:]], axis=0)
    energy = real_part * real_part + imag_part * imag_part
    sums = jnp.sum(energy, axis=1, keepdims=True)
    sums = sums[:rows] + sums[rows:]
    spread = jnp.dot(energy.astype(jnp.bfloat16), env[...], preferred_element_type=jnp.float32)
    spread = spread[:rows] + spread[rows:] * parity_row(1, 2 * FB)
    factor = 1.0 / (math.sqrt(SAMPLES) * (sums / SAMPLES + epsilon))
    e_tab[...] = (spread * factor).astype(jnp.bfloat16).astype(jnp.float32)

    for r in range(3, rounds):
        hear(r)

    def outgoing(dest):
        return pltpu.make_async_remote_copy(
            src_ref=send_buf.at[dest],
            dst_ref=recv_buf.at[me],
            send_sem=send_sem.at[dest],
            recv_sem=recv_sem.at[me],
            device_id={"chan": dest},
            device_id_type=MESH,
        )

    def send_pair(step):
        for side in range(PAIR):
            dest = pair_at(step) * PAIR + side

            @pl.when(dest != me)
            def _():
                outgoing(dest).start()

    @pl.loop(0, pairs)
    def _(step):
        @pl.when(step >= ahead)
        def _():
            phases(step)

        pair = pair_at(step)
        at = pl.ds(pl.multiple_of(pair * block, block), block)
        acc = [[jnp.zeros((block, FB), jnp.float32) for _ in range(kept)] for _ in range(2)]
        for ch in range(chans):
            pc = phase_c[ch, at, :].astype(jnp.float32)
            ps = phase_s[ch, at, :].astype(jnp.float32)
            for w in range(kept):
                r = w * chans + ch
                er, ei = e_tab[r : r + 1, :FB], e_tab[r : r + 1, FB:]
                acc[0][w] = acc[0][w] + (pc * er - ps * ei)
                acc[1][w] = acc[1][w] + (pc * ei + ps * er)
        for side in range(PAIR):
            part = slice(side * node_rows, (side + 1) * node_rows)
            packed = jnp.concatenate([acc[p][w][part] for p in range(2) for w in range(kept)], axis=0)
            send_buf[pair * PAIR + side] = packed.astype(jnp.bfloat16)

        @pl.when(step > 0)
        def _():
            send_pair(step - 1)

    send_pair(pairs - 1)

    def incoming(source):
        return pltpu.make_async_remote_copy(
            src_ref=send_buf.at[source],
            dst_ref=recv_buf.at[source],
            send_sem=send_sem.at[source],
            recv_sem=recv_sem.at[source],
            device_id={"chan": source},
            device_id_type=MESH,
        )

    def add_one(source, stack):
        incoming(source).wait_recv()
        return stack + recv_buf[source].astype(jnp.float32)

    def add_pair(step, stack):
        for side in range(PAIR):
            stack = add_one(pair_at(step) * PAIR + side, stack)
        return stack

    stack = lax.fori_loop(0, pairs - 1, add_pair, send_buf[me].astype(jnp.float32))
    stack = add_one(flip(me, 0), stack)

    turned = []
    for w in range(kept):
        c, s = turn_row[w, :, :FB], turn_row[w, :, FB:]
        re = stack[w * node_rows : (w + 1) * node_rows]
        im = stack[(kept + w) * node_rows : (kept + w + 1) * node_rows]
        turned.append(jnp.concatenate([re * c - im * s, re * s + im * c], axis=1))
    bright = jnp.dot(
        jnp.concatenate(turned, axis=0), turn_tab[...],
        precision=lax.Precision.HIGHEST, preferred_element_type=jnp.float32,
    )
    scale = 1.0 / math.sqrt(FB * chans * n_chan)
    out_ref[...] = (bright * scale).reshape(kept, node_rows, TB)

    @pl.loop(1, n_chan)
    def _(step):
        outgoing(lax.rem(me + step, n_chan)).wait_send()


def solution(mesh):
    n_chan = mesh.shape["chan"]

    def on_device(traces, delays, offsets):
        chans, windows, half = traces.shape
        nodes = delays.shape[0]
        kept = offsets.shape[0]
        node_rows = nodes // n_chan
        by_window = jnp.transpose(traces, (1, 0, 2))
        vmem = pl.BlockSpec(memory_space=pltpu.VMEM)
        packed_rows = 2 * kept * node_rows
        return pl.pallas_call(
            functools.partial(kernel, n_chan),
            out_shape=jax.ShapeDtypeStruct((kept, node_rows, TB), jnp.float32),
            in_specs=[vmem, vmem, pl.BlockSpec(memory_space=pltpu.HBM)],
            out_specs=vmem,
            scratch_shapes=[
                pltpu.VMEM((kept, chans, half), jnp.bfloat16),
                pltpu.VMEM((STEP, BAND + FB), jnp.float32),
                pltpu.VMEM((STEP, BAND + FB), jnp.float32),
                pltpu.VMEM(((BAND + FB) // 128, half // STEP, 128), jnp.float32),
                pltpu.VMEM(((BAND + FB) // 128, half // STEP, 128), jnp.float32),
                pltpu.VMEM((half, 2 * BAND), jnp.bfloat16),
                pltpu.VMEM((half, 2 * BAND), jnp.bfloat16),
                pltpu.VMEM((half, 2 * FB), jnp.bfloat16),
                pltpu.VMEM((chans, nodes, FB), jnp.bfloat16),
                pltpu.VMEM((chans, nodes, FB), jnp.bfloat16),
                pltpu.VMEM((nodes, chans), jnp.float32),
                pltpu.VMEM((2 * FB, TB), jnp.float32),
                pltpu.VMEM((kept, 1, 2 * FB), jnp.float32),
                pltpu.VMEM((kept * chans, 2 * FB), jnp.float32),
                pltpu.VMEM((n_chan, packed_rows, FB), jnp.bfloat16),
                pltpu.VMEM((n_chan, packed_rows, FB), jnp.bfloat16),
                pltpu.SMEM((kept,), jnp.int32),
                pltpu.SemaphoreType.DMA,
                pltpu.SemaphoreType.DMA,
                pltpu.SemaphoreType.DMA,
                pltpu.SemaphoreType.DMA((n_chan,)),
                pltpu.SemaphoreType.DMA((n_chan,)),
                pltpu.SemaphoreType.REGULAR((n_chan.bit_length() - 1,)),
            ],
            compiler_params=pltpu.CompilerParams(
                collective_id=0, has_side_effects=True, vmem_limit_bytes=16 * 1024 * 1024 + 4 * chans * nodes * FB
            ),
        )(by_window, delays.T, offsets)

    placed = (P("chan", None, "tm"), P(None, "chan"), P("tm"))
    return jax.shard_map(
        on_device, mesh=mesh, in_specs=placed, out_specs=P("tm", "chan", None), check_vma=False
    )
```

```python
import functools
import math

import jax
import jax.numpy as jnp
from jax import lax
from jax.experimental import pallas as pl
from jax.experimental.pallas import tpu as pltpu
from jax.sharding import PartitionSpec as P

SAMPLES = 2048
BAND = 512
FB = 128
TB = 256
BAND_LO = 128
DEC = 8
STEP = 32
PAIR = 2

epsilon = 1e-06
full_turn = 2.0 * math.pi
MESH = pl.DeviceIdType.MESH


COS_TURN = (
    0.9999999890590201, -19.739204499453688, 64.93911745988827, -85.45013953077586,
    60.16763095018129, -25.96759924584206, 6.528658157862129,
)
SIN_TURN = (
    6.283185302511498, -41.341700405316736, 81.60513138576982, -76.70301535347629,
    42.02592698341473, -14.899846660399582, 3.2381375010236435,
)


def cos_sin(turns):
    x = turns - jnp.round(turns)
    y = x * x
    c, s = COS_TURN[-1], SIN_TURN[-1]
    for c_next, s_next in zip(COS_TURN[-2::-1], SIN_TURN[-2::-1]):
        c = c * y + c_next
        s = s * y + s_next
    return c, s * x


def float_iota(shape, axis):
    return lax.broadcasted_iota(jnp.int32, shape, axis).astype(jnp.float32)


def bit_of(value, at):
    return lax.rem(value // (1 << at), 2)


def flip(value, at):
    return value + (1 - 2 * bit_of(value, at)) * (1 << at)


def parity_row(first, width):
    ids = first + lax.broadcasted_iota(jnp.int32, (1, width), 1)
    return (1 - 2 * (ids & 1)).astype(jnp.float32)


def kernel(
    n_chan, x_hbm, d_hbm, off_hbm, out_ref,
    x_ref, d_ref, other, all_rows, base_c, base_s, lead_c, lead_s, fwd, inv, env, phase_c, phase_s,
    nodes_d, turn_tab, turn_row, e_tab, send_buf, recv_buf,
    off_ref, off_sem, x_sem, d_sem, x_send, x_recv, send_sem, recv_sem, round_sem,
):
    chans, windows, half = x_hbm.shape
    kept = windows // 2
    rows = kept * chans
    nodes = d_hbm.shape[1]
    node_rows = nodes // n_chan
    me = lax.axis_index("chan")
    tm = lax.axis_index("tm")
    partner = 1 - tm

    offsets_in = pltpu.make_async_copy(off_hbm, off_ref, off_sem)
    samples_in = pltpu.make_async_copy(x_hbm, x_ref, x_sem)
    delays_in = pltpu.make_async_copy(d_hbm, d_ref, d_sem)
    samples_in.start()
    delays_in.start()
    offsets_in.start()

    rounds = n_chan.bit_length() - 1
    barrier = pltpu.get_barrier_semaphore()
    pl.semaphore_signal(barrier, inc=1, device_id={"tm": partner}, device_id_type=MESH)
    for r in range(rounds):
        pl.semaphore_signal(barrier, inc=1, device_id={"chan": flip(me, r)}, device_id_type=MESH)

    def tell(r):
        if r < rounds:
            pl.semaphore_signal(round_sem.at[r], inc=1, device_id={"chan": flip(me, r)}, device_id_type=MESH)

    def hear(r):
        if r < rounds:
            pl.semaphore_wait(round_sem.at[r], 1)
            tell(r + 1)

    width = BAND + FB
    tiles = BAND // 128
    side_tiles = tiles // 2
    side_band = BAND // 2
    leads = half // STEP
    unit = 1.0 / SAMPLES
    for q in range(width // 128):
        cols = slice(q * 128, (q + 1) * 128)
        if q < tiles:
            freq = (2.0 * float_iota((1, 128), 1) + (BAND_LO + q % side_tiles * 256 + q // side_tiles)) * unit
        else:
            freq = (float_iota((1, 128), 1) + (1 + (q - tiles) * 128)) * unit
        base_c[:, cols], base_s[:, cols] = cos_sin(float_iota((STEP, 128), 0) * freq)
        lead_c[q], lead_s[q] = cos_sin(float_iota((leads, 128), 0) * (freq * STEP))

    place = float_iota((1, side_band), 1) * 2.0
    place = jnp.concatenate([place, place + 1.0], axis=1)
    taper_angle = math.pi * (place + 0.5) / BAND
    weight = 2.0 * jnp.sin(taper_angle) ** 2 / SAMPLES

    pl.semaphore_wait(barrier, rounds + 1)
    exchange = pltpu.make_async_remote_copy(
        src_ref=x_hbm,
        dst_ref=other,
        send_sem=x_send,
        recv_sem=x_recv,
        device_id={"tm": partner},
        device_id_type=MESH,
    )
    exchange.start()

    tell(0)

    @pl.loop(0, half // STEP)
    def _(a):
        at = pl.ds(pl.multiple_of(a * STEP, STEP), STEP)
        for q in range(width // 128):
            cols = slice(q * 128, (q + 1) * 128)
            ca, sa = lead_c[q, pl.ds(a, 1), :], lead_s[q, pl.ds(a, 1), :]
            cb, sb = base_c[:, cols], base_s[:, cols]
            c = ca * cb - sa * sb
            s = sa * cb + ca * sb
            if q * 128 < BAND:
                g = weight[:, cols]
                high = slice(BAND + q * 128, BAND + (q + 1) * 128)
                fwd[at, cols] = c.astype(jnp.bfloat16)
                fwd[at, high] = (-s).astype(jnp.bfloat16)
                to = q // side_tiles * BAND + q % side_tiles * 128
                inv[at, to : to + 128] = (g * c).astype(jnp.bfloat16)
                inv[at, to + side_band : to + side_band + 128] = (g * s).astype(jnp.bfloat16)
            else:
                low = slice(q * 128 - BAND, (q + 1) * 128 - BAND)
                high = slice(FB + low.start, FB + low.stop)
                env[at, low] = c.astype(jnp.bfloat16)
                env[at, high] = (-s).astype(jnp.bfloat16)

    hear(0)

    delays_in.wait()
    nodes_d[...] = (d_ref[...].astype(jnp.float32) * unit).T
    block = PAIR * node_rows
    env_bins = 1.0 + float_iota((1, FB), 1)

    pairs = n_chan // PAIR
    ahead = (pairs + 1) // 2
    my_pair = me // PAIR

    def pair_at(step):
        mask = pairs - 1 - step
        found = 0
        for at in range(rounds - 1):
            found = found + lax.rem(bit_of(my_pair, at) + bit_of(mask, at), 2) * (1 << at)
        return found

    def phases(step):
        at = pl.ds(pl.multiple_of(pair_at(step) * block, block), block)
        delay = nodes_d[at, :]
        for ch in range(chans):
            c, s = cos_sin(delay[:, ch : ch + 1] * env_bins)
            phase_c[ch, at, :] = c.astype(jnp.bfloat16)
            phase_s[ch, at, :] = s.astype(jnp.bfloat16)

    pl.loop(0, ahead)(phases)
    hear(1)
    c, s = cos_sin((1.0 + float_iota((FB, TB), 0)) * (float_iota((FB, TB), 1) * (DEC * unit)))
    turn_tab[:FB, :] = c
    turn_tab[FB:, :] = -s
    offsets_in.wait()
    for w in range(kept):
        shift = off_ref[w].astype(jnp.float32) * unit
        turn_row[w, :, :FB], turn_row[w, :, FB:] = cos_sin(env_bins * shift)
    hear(2)

    def kept_terms(samples):
        terms = jnp.dot(samples.reshape(chans * windows, half), fwd[...], preferred_element_type=jnp.float32)
        cols = []
        for q in range(2 * BAND // 128):
            all_rows[q] = terms[:, q * 128 : (q + 1) * 128]
            picked = []
            for w in range(kept):
                early = all_rows[q, pl.ds(w, chans, stride=windows), :]
                late = all_rows[q, pl.ds(kept + w, chans, stride=windows), :]
                picked.append(jnp.where(is_late, late, early))
            cols.append(jnp.concatenate(picked, axis=0))
        return jnp.concatenate(cols, axis=1)

    is_late = (lax.broadcasted_iota(jnp.int32, (1, 128), 1) * 0 + tm) == 1
    samples_in.wait()
    own_terms = kept_terms(x_ref[...])
    exchange.wait()
    other_terms = kept_terms(other[...])
    late_sign = jnp.where((lax.broadcasted_iota(jnp.int32, (1, side_band), 1) * 0 + tm) == 1, -1.0, 1.0)

    def spectrum(first, odd):
        cols = slice(first, first + side_band)
        mine, theirs = own_terms[:, cols], other_terms[:, cols]
        both = (mine - theirs) * late_sign if odd else mine + theirs
        return both.astype(jnp.bfloat16).astype(jnp.float32)

    def analytic(odd):
        re, im = spectrum(odd * side_band, odd), spectrum(BAND + odd * side_band, odd)
        left = jnp.concatenate([re, im], axis=0)
        right = jnp.concatenate([-im, re], axis=0)
        return lax.dot_general(
            jnp.concatenate([left, right], axis=1).astype(jnp.bfloat16),
            inv[:, odd * BAND : (odd + 1) * BAND],
            (((1,), (1,)), ((), ())),
            preferred_element_type=jnp.float32,
        )

    even_part, odd_part = analytic(0), analytic(1)
    early, late = even_part + odd_part, even_part - odd_part
    real_part = jnp.concatenate([early[:rows], late[:rows]], axis=0)
    imag_part = jnp.concatenate([early[rows:], late[rows:]], axis=0)
    energy = real_part * real_part + imag_part * imag_part
    sums = jnp.sum(energy, axis=1, keepdims=True)
    sums = sums[:rows] + sums[rows:]
    spread = jnp.dot(energy.astype(jnp.bfloat16), env[...], preferred_element_type=jnp.float32)
    spread = spread[:rows] + spread[rows:] * parity_row(1, 2 * FB)
    factor = 1.0 / (math.sqrt(SAMPLES) * (sums / SAMPLES + epsilon))
    e_tab[...] = (spread * factor).astype(jnp.bfloat16).astype(jnp.float32)

    for r in range(3, rounds):
        hear(r)

    def outgoing(dest):
        return pltpu.make_async_remote_copy(
            src_ref=send_buf.at[dest],
            dst_ref=recv_buf.at[me],
            send_sem=send_sem.at[dest],
            recv_sem=recv_sem.at[me],
            device_id={"chan": dest},
            device_id_type=MESH,
        )

    def send_pair(step):
        for side in range(PAIR):
            dest = pair_at(step) * PAIR + side

            @pl.when(dest != me)
            def _():
                outgoing(dest).start()

    @pl.loop(0, pairs)
    def _(step):
        @pl.when(step >= ahead)
        def _():
            phases(step)

        pair = pair_at(step)
        at = pl.ds(pl.multiple_of(pair * block, block), block)
        acc = [[jnp.zeros((block, FB), jnp.float32) for _ in range(kept)] for _ in range(2)]
        for ch in range(chans):
            pc = phase_c[ch, at, :].astype(jnp.float32)
            ps = phase_s[ch, at, :].astype(jnp.float32)
            for w in range(kept):
                r = w * chans + ch
                er, ei = e_tab[r : r + 1, :FB], e_tab[r : r + 1, FB:]
                acc[0][w] = acc[0][w] + (pc * er - ps * ei)
                acc[1][w] = acc[1][w] + (pc * ei + ps * er)
        for side in range(PAIR):
            part = slice(side * node_rows, (side + 1) * node_rows)
            packed = jnp.concatenate([acc[p][w][part] for p in range(2) for w in range(kept)], axis=0)
            send_buf[pair * PAIR + side] = packed.astype(jnp.bfloat16)

        @pl.when(step > 0)
        def _():
            send_pair(step - 1)

    send_pair(pairs - 1)

    def incoming(source):
        return pltpu.make_async_remote_copy(
            src_ref=send_buf.at[source],
            dst_ref=recv_buf.at[source],
            send_sem=send_sem.at[source],
            recv_sem=recv_sem.at[source],
            device_id={"chan": source},
            device_id_type=MESH,
        )

    def add_one(source, stack):
        incoming(source).wait_recv()
        return stack + recv_buf[source].astype(jnp.float32)

    def add_pair(step, stack):
        for side in range(PAIR):
            stack = add_one(pair_at(step) * PAIR + side, stack)
        return stack

    stack = lax.fori_loop(0, pairs - 1, add_pair, send_buf[me].astype(jnp.float32))
    stack = add_one(flip(me, 0), stack)

    turned = []
    for w in range(kept):
        c, s = turn_row[w, :, :FB], turn_row[w, :, FB:]
        re = stack[w * node_rows : (w + 1) * node_rows]
        im = stack[(kept + w) * node_rows : (kept + w + 1) * node_rows]
        turned.append(jnp.concatenate([re * c - im * s, re * s + im * c], axis=1))
    bright = jnp.dot(
        jnp.concatenate(turned, axis=0), turn_tab[...],
        precision=lax.Precision.HIGHEST, preferred_element_type=jnp.float32,
    )
    scale = 1.0 / math.sqrt(FB * chans * n_chan)
    out_ref[...] = (bright * scale).reshape(kept, node_rows, TB)

    @pl.loop(1, n_chan)
    def _(step):
        outgoing(lax.rem(me + step, n_chan)).wait_send()


def solution(mesh):
    n_chan = mesh.shape["chan"]

    def on_device(traces, delays, offsets):
        chans, windows, half = traces.shape
        nodes = delays.shape[0]
        kept = offsets.shape[0]
        node_rows = nodes // n_chan
        vmem = pl.BlockSpec(memory_space=pltpu.VMEM)
        packed_rows = 2 * kept * node_rows
        return pl.pallas_call(
            functools.partial(kernel, n_chan),
            out_shape=jax.ShapeDtypeStruct((kept, node_rows, TB), jnp.float32),
            in_specs=[pl.BlockSpec(memory_space=pltpu.HBM)] * 3,
            out_specs=vmem,
            scratch_shapes=[
                pltpu.VMEM((chans, windows, half), jnp.bfloat16),
                pltpu.VMEM((chans, nodes), jnp.int32),
                pltpu.VMEM((chans, windows, half), jnp.bfloat16),
                pltpu.VMEM((2 * BAND // 128, chans * windows, 128), jnp.float32),
                pltpu.VMEM((STEP, BAND + FB), jnp.float32),
                pltpu.VMEM((STEP, BAND + FB), jnp.float32),
                pltpu.VMEM(((BAND + FB) // 128, half // STEP, 128), jnp.float32),
                pltpu.VMEM(((BAND + FB) // 128, half // STEP, 128), jnp.float32),
                pltpu.VMEM((half, 2 * BAND), jnp.bfloat16),
                pltpu.VMEM((half, 2 * BAND), jnp.bfloat16),
                pltpu.VMEM((half, 2 * FB), jnp.bfloat16),
                pltpu.VMEM((chans, nodes, FB), jnp.bfloat16),
                pltpu.VMEM((chans, nodes, FB), jnp.bfloat16),
                pltpu.VMEM((nodes, chans), jnp.float32),
                pltpu.VMEM((2 * FB, TB), jnp.float32),
                pltpu.VMEM((kept, 1, 2 * FB), jnp.float32),
                pltpu.VMEM((kept * chans, 2 * FB), jnp.float32),
                pltpu.VMEM((n_chan, packed_rows, FB), jnp.bfloat16),
                pltpu.VMEM((n_chan, packed_rows, FB), jnp.bfloat16),
                pltpu.SMEM((kept,), jnp.int32),
                pltpu.SemaphoreType.DMA,
                pltpu.SemaphoreType.DMA,
                pltpu.SemaphoreType.DMA,
                pltpu.SemaphoreType.DMA,
                pltpu.SemaphoreType.DMA,
                pltpu.SemaphoreType.DMA((n_chan,)),
                pltpu.SemaphoreType.DMA((n_chan,)),
                pltpu.SemaphoreType.REGULAR((n_chan.bit_length() - 1,)),
            ],
            compiler_params=pltpu.CompilerParams(
                collective_id=0, has_side_effects=True, vmem_limit_bytes=16 * 1024 * 1024 + 4 * chans * nodes * FB
            ),
        )(*(pltpu.with_memory_space_constraint(a, pltpu.HBM) for a in (traces, delays.T, offsets)))

    placed = (P("chan", None, "tm"), P(None, "chan"), P("tm"))
    return jax.shard_map(
        on_device, mesh=mesh, in_specs=placed, out_specs=P("tm", "chan", None), check_vma=False
    )
```

```python
import functools
import math

import jax
import jax.numpy as jnp
from jax import lax
from jax.experimental import pallas as pl
from jax.experimental.pallas import tpu as pltpu
from jax.sharding import PartitionSpec as P

SAMPLES = 2048
BAND = 512
FB = 128
TB = 256
BAND_LO = 128
DEC = 8
STEP = 32
PAIR = 2

epsilon = 1e-06
full_turn = 2.0 * math.pi
MESH = pl.DeviceIdType.MESH


COS_TURN = (
    0.9999999890590201, -19.739204499453688, 64.93911745988827, -85.45013953077586,
    60.16763095018129, -25.96759924584206, 6.528658157862129,
)
SIN_TURN = (
    6.283185302511498, -41.341700405316736, 81.60513138576982, -76.70301535347629,
    42.02592698341473, -14.899846660399582, 3.2381375010236435,
)


def cos_sin(turns):
    x = turns - jnp.round(turns)
    y = x * x
    c, s = COS_TURN[-1], SIN_TURN[-1]
    for c_next, s_next in zip(COS_TURN[-2::-1], SIN_TURN[-2::-1]):
        c = c * y + c_next
        s = s * y + s_next
    return c, s * x


def float_iota(shape, axis):
    return lax.broadcasted_iota(jnp.int32, shape, axis).astype(jnp.float32)


def bit_of(value, at):
    return lax.rem(value // (1 << at), 2)


def flip(value, at):
    return value + (1 - 2 * bit_of(value, at)) * (1 << at)


def parity_row(first, width):
    ids = first + lax.broadcasted_iota(jnp.int32, (1, width), 1)
    return (1 - 2 * (ids & 1)).astype(jnp.float32)


def kernel(
    n_chan, x_ref, d_hbm, off_hbm, out_ref,
    d_ref, other, base_c, base_s, lead_c, lead_s, fwd, inv, env, phase_c, phase_s,
    nodes_d, turn_tab, turn_row, e_tab, send_buf, recv_buf,
    off_ref, off_sem, d_sem, x_send, x_recv, send_sem, recv_sem, round_sem,
):
    windows, chans, half = x_ref.shape
    kept = windows // 2
    rows = kept * chans
    nodes = d_hbm.shape[1]
    node_rows = nodes // n_chan
    me = lax.axis_index("chan")
    tm = lax.axis_index("tm")
    partner = 1 - tm

    offsets_in = pltpu.make_async_copy(off_hbm, off_ref, off_sem)
    delays_in = pltpu.make_async_copy(d_hbm, d_ref, d_sem)
    delays_in.start()
    offsets_in.start()

    rounds = n_chan.bit_length() - 1
    barrier = pltpu.get_barrier_semaphore()
    pl.semaphore_signal(barrier, inc=1, device_id={"tm": partner}, device_id_type=MESH)
    for r in range(rounds):
        pl.semaphore_signal(barrier, inc=1, device_id={"chan": flip(me, r)}, device_id_type=MESH)

    def tell(r):
        if r < rounds:
            pl.semaphore_signal(round_sem.at[r], inc=1, device_id={"chan": flip(me, r)}, device_id_type=MESH)

    def hear(r):
        if r < rounds:
            pl.semaphore_wait(round_sem.at[r], 1)
            tell(r + 1)

    width = BAND + FB
    tiles = BAND // 128
    side_tiles = tiles // 2
    side_band = BAND // 2
    leads = half // STEP
    unit = 1.0 / SAMPLES
    for q in range(width // 128):
        cols = slice(q * 128, (q + 1) * 128)
        if q < tiles:
            freq = (2.0 * float_iota((1, 128), 1) + (BAND_LO + q % side_tiles * 256 + q // side_tiles)) * unit
        else:
            freq = (float_iota((1, 128), 1) + (1 + (q - tiles) * 128)) * unit
        base_c[:, cols], base_s[:, cols] = cos_sin(float_iota((STEP, 128), 0) * freq)
        lead_c[q], lead_s[q] = cos_sin(float_iota((leads, 128), 0) * (freq * STEP))

    place = float_iota((1, side_band), 1) * 2.0
    place = jnp.concatenate([place, place + 1.0], axis=1)
    taper_angle = math.pi * (place + 0.5) / BAND
    weight = 2.0 * jnp.sin(taper_angle) ** 2 / SAMPLES

    pl.semaphore_wait(barrier, rounds + 1)
    exchange = pltpu.make_async_remote_copy(
        src_ref=x_ref.at[pl.ds(partner * kept, kept)],
        dst_ref=other,
        send_sem=x_send,
        recv_sem=x_recv,
        device_id={"tm": partner},
        device_id_type=MESH,
    )
    exchange.start()

    tell(0)

    @pl.loop(0, half // STEP)
    def _(a):
        at = pl.ds(pl.multiple_of(a * STEP, STEP), STEP)
        for q in range(width // 128):
            cols = slice(q * 128, (q + 1) * 128)
            ca, sa = lead_c[q, pl.ds(a, 1), :], lead_s[q, pl.ds(a, 1), :]
            cb, sb = base_c[:, cols], base_s[:, cols]
            c = ca * cb - sa * sb
            s = sa * cb + ca * sb
            if q * 128 < BAND:
                g = weight[:, cols]
                high = slice(BAND + q * 128, BAND + (q + 1) * 128)
                fwd[at, cols] = c.astype(jnp.bfloat16)
                fwd[at, high] = (-s).astype(jnp.bfloat16)
                to = q // side_tiles * BAND + q % side_tiles * 128
                inv[at, to : to + 128] = (g * c).astype(jnp.bfloat16)
                inv[at, to + side_band : to + side_band + 128] = (g * s).astype(jnp.bfloat16)
            else:
                low = slice(q * 128 - BAND, (q + 1) * 128 - BAND)
                high = slice(FB + low.start, FB + low.stop)
                env[at, low] = c.astype(jnp.bfloat16)
                env[at, high] = (-s).astype(jnp.bfloat16)

    hear(0)

    delays_in.wait()
    nodes_d[...] = (d_ref[...].astype(jnp.float32) * unit).T
    block = PAIR * node_rows
    env_bins = 1.0 + float_iota((1, FB), 1)

    pairs = n_chan // PAIR
    ahead = (pairs + 1) // 2
    my_pair = me // PAIR

    def pair_at(step):
        mask = pairs - 1 - step
        found = 0
        for at in range(rounds - 1):
            found = found + lax.rem(bit_of(my_pair, at) + bit_of(mask, at), 2) * (1 << at)
        return found

    def phases(step):
        at = pl.ds(pl.multiple_of(pair_at(step) * block, block), block)
        delay = nodes_d[at, :]
        for ch in range(chans):
            c, s = cos_sin(delay[:, ch : ch + 1] * env_bins)
            phase_c[ch, at, :] = c.astype(jnp.bfloat16)
            phase_s[ch, at, :] = s.astype(jnp.bfloat16)

    pl.loop(0, ahead)(phases)
    hear(1)
    hear(2)

    own = x_ref[pl.ds(tm * kept, kept)].reshape(rows, half)
    own_terms = jnp.dot(own, fwd[...], preferred_element_type=jnp.float32)
    exchange.wait()
    other_terms = jnp.dot(other[...].reshape(rows, half), fwd[...], preferred_element_type=jnp.float32)
    late_sign = jnp.where((lax.broadcasted_iota(jnp.int32, (1, side_band), 1) * 0 + tm) == 1, -1.0, 1.0)

    def spectrum(first, odd):
        cols = slice(first, first + side_band)
        mine, theirs = own_terms[:, cols], other_terms[:, cols]
        both = (mine - theirs) * late_sign if odd else mine + theirs
        return both.astype(jnp.bfloat16).astype(jnp.float32)

    def analytic(odd):
        re, im = spectrum(odd * side_band, odd), spectrum(BAND + odd * side_band, odd)
        left = jnp.concatenate([re, im], axis=0)
        right = jnp.concatenate([-im, re], axis=0)
        return lax.dot_general(
            jnp.concatenate([left, right], axis=1).astype(jnp.bfloat16),
            inv[:, odd * BAND : (odd + 1) * BAND],
            (((1,), (1,)), ((), ())),
            preferred_element_type=jnp.float32,
        )

    even_part, odd_part = analytic(0), analytic(1)
    early, late = even_part + odd_part, even_part - odd_part
    real_part = jnp.concatenate([early[:rows], late[:rows]], axis=0)
    imag_part = jnp.concatenate([early[rows:], late[rows:]], axis=0)
    energy = real_part * real_part + imag_part * imag_part
    sums = jnp.sum(energy, axis=1, keepdims=True)
    sums = sums[:rows] + sums[rows:]
    spread = jnp.dot(energy.astype(jnp.bfloat16), env[...], preferred_element_type=jnp.float32)
    spread = spread[:rows] + spread[rows:] * parity_row(1, 2 * FB)
    factor = 1.0 / (math.sqrt(SAMPLES) * (sums / SAMPLES + epsilon))
    e_tab[...] = (spread * factor).astype(jnp.bfloat16).astype(jnp.float32)

    for r in range(3, rounds):
        hear(r)

    def outgoing(dest):
        return pltpu.make_async_remote_copy(
            src_ref=send_buf.at[dest],
            dst_ref=recv_buf.at[me],
            send_sem=send_sem.at[dest],
            recv_sem=recv_sem.at[me],
            device_id={"chan": dest},
            device_id_type=MESH,
        )

    def send_pair(step):
        for side in range(PAIR):
            dest = pair_at(step) * PAIR + side

            @pl.when(dest != me)
            def _():
                outgoing(dest).start()

    @pl.loop(0, pairs)
    def _(step):
        @pl.when(step >= ahead)
        def _():
            phases(step)

        pair = pair_at(step)
        at = pl.ds(pl.multiple_of(pair * block, block), block)
        acc = [[jnp.zeros((block, FB), jnp.float32) for _ in range(kept)] for _ in range(2)]
        for ch in range(chans):
            pc = phase_c[ch, at, :].astype(jnp.float32)
            ps = phase_s[ch, at, :].astype(jnp.float32)
            for w in range(kept):
                r = w * chans + ch
                er, ei = e_tab[r : r + 1, :FB], e_tab[r : r + 1, FB:]
                acc[0][w] = acc[0][w] + (pc * er - ps * ei)
                acc[1][w] = acc[1][w] + (pc * ei + ps * er)
        for side in range(PAIR):
            part = slice(side * node_rows, (side + 1) * node_rows)
            packed = jnp.concatenate([acc[p][w][part] for p in range(2) for w in range(kept)], axis=0)
            send_buf[pair * PAIR + side] = packed.astype(jnp.bfloat16)

        @pl.when(step > 0)
        def _():
            send_pair(step - 1)

    send_pair(pairs - 1)

    c, s = cos_sin((1.0 + float_iota((FB, TB), 0)) * (float_iota((FB, TB), 1) * (DEC * unit)))
    turn_tab[:FB, :] = c
    turn_tab[FB:, :] = -s
    offsets_in.wait()
    for w in range(kept):
        shift = off_ref[w].astype(jnp.float32) * unit
        turn_row[w, :, :FB], turn_row[w, :, FB:] = cos_sin(env_bins * shift)

    def incoming(source):
        return pltpu.make_async_remote_copy(
            src_ref=send_buf.at[source],
            dst_ref=recv_buf.at[source],
            send_sem=send_sem.at[source],
            recv_sem=recv_sem.at[source],
            device_id={"chan": source},
            device_id_type=MESH,
        )

    def add_one(source, stack):
        incoming(source).wait_recv()
        return stack + recv_buf[source].astype(jnp.float32)

    def add_pair(step, stack):
        for side in range(PAIR):
            stack = add_one(pair_at(step) * PAIR + side, stack)
        return stack

    stack = lax.fori_loop(0, pairs - 1, add_pair, send_buf[me].astype(jnp.float32))
    stack = add_one(flip(me, 0), stack)

    turned = []
    for w in range(kept):
        c, s = turn_row[w, :, :FB], turn_row[w, :, FB:]
        re = stack[w * node_rows : (w + 1) * node_rows]
        im = stack[(kept + w) * node_rows : (kept + w + 1) * node_rows]
        turned.append(jnp.concatenate([re * c - im * s, re * s + im * c], axis=1))
    bright = jnp.dot(
        jnp.concatenate(turned, axis=0), turn_tab[...],
        precision=lax.Precision.HIGHEST, preferred_element_type=jnp.float32,
    )
    scale = 1.0 / math.sqrt(FB * chans * n_chan)
    out_ref[...] = (bright * scale).reshape(kept, node_rows, TB)

    @pl.loop(1, n_chan)
    def _(step):
        outgoing(lax.rem(me + step, n_chan)).wait_send()


def solution(mesh):
    n_chan = mesh.shape["chan"]

    def on_device(traces, delays, offsets):
        chans, windows, half = traces.shape
        nodes = delays.shape[0]
        kept = offsets.shape[0]
        node_rows = nodes // n_chan
        by_window = jnp.transpose(traces, (1, 0, 2))
        vmem = pl.BlockSpec(memory_space=pltpu.VMEM)
        packed_rows = 2 * kept * node_rows
        return pl.pallas_call(
            functools.partial(kernel, n_chan),
            out_shape=jax.ShapeDtypeStruct((kept, node_rows, TB), jnp.float32),
            in_specs=[vmem] + [pl.BlockSpec(memory_space=pltpu.HBM)] * 2,
            out_specs=vmem,
            scratch_shapes=[
                pltpu.VMEM((chans, nodes), jnp.int32),
                pltpu.VMEM((kept, chans, half), jnp.bfloat16),
                pltpu.VMEM((STEP, BAND + FB), jnp.float32),
                pltpu.VMEM((STEP, BAND + FB), jnp.float32),
                pltpu.VMEM(((BAND + FB) // 128, half // STEP, 128), jnp.float32),
                pltpu.VMEM(((BAND + FB) // 128, half // STEP, 128), jnp.float32),
                pltpu.VMEM((half, 2 * BAND), jnp.bfloat16),
                pltpu.VMEM((half, 2 * BAND), jnp.bfloat16),
                pltpu.VMEM((half, 2 * FB), jnp.bfloat16),
                pltpu.VMEM((chans, nodes, FB), jnp.bfloat16),
                pltpu.VMEM((chans, nodes, FB), jnp.bfloat16),
                pltpu.VMEM((nodes, chans), jnp.float32),
                pltpu.VMEM((2 * FB, TB), jnp.float32),
                pltpu.VMEM((kept, 1, 2 * FB), jnp.float32),
                pltpu.VMEM((kept * chans, 2 * FB), jnp.float32),
                pltpu.VMEM((n_chan, packed_rows, FB), jnp.bfloat16),
                pltpu.VMEM((n_chan, packed_rows, FB), jnp.bfloat16),
                pltpu.SMEM((kept,), jnp.int32),
                pltpu.SemaphoreType.DMA,
                pltpu.SemaphoreType.DMA,
                pltpu.SemaphoreType.DMA,
                pltpu.SemaphoreType.DMA,
                pltpu.SemaphoreType.DMA((n_chan,)),
                pltpu.SemaphoreType.DMA((n_chan,)),
                pltpu.SemaphoreType.REGULAR((n_chan.bit_length() - 1,)),
            ],
            compiler_params=pltpu.CompilerParams(
                collective_id=0, has_side_effects=True, vmem_limit_bytes=16 * 1024 * 1024 + 4 * chans * nodes * FB
            ),
        )(by_window, *(pltpu.with_memory_space_constraint(a, pltpu.HBM) for a in (delays.T, offsets)))

    placed = (P("chan", None, "tm"), P(None, "chan"), P("tm"))
    return jax.shard_map(
        on_device, mesh=mesh, in_specs=placed, out_specs=P("tm", "chan", None), check_vma=False
    )
```
